512 devices in a mesh: row: 32 (over z, y_lo), col: 16 (over y_hi, x, core).
Axes of the slice: x: 4, y: 8 (y_hi: 2, y_lo: 4; y = y_hi * 4 + y_lo), z: 8, core: 2. Of those that a mesh axis runs over, the one named last changes fastest.
Arguments:
- features: bfloat16 [16, 4096, 128], P('col', 'row'), may hold values from -6 to 6
- weight1: bfloat16 [128, 128], replicated, may hold values from -0.5 to 0.5
- weight2: bfloat16 [128, 128], replicated, may hold values from -0.5 to 0.5
- tile_values: bfloat16 [32, 16, 96, 128, 128], P('row', 'col'), may hold values from -0.1875 to 0.1875
- tile_coords: int32 [32, 16, 2, 96], P('row', 'col'), may hold values from 0 to 31, as said below
- tile_count: int32 [32, 16], P('row', 'col'), may hold values from 1 to 96, as said below
- out_grad: bfloat16 [16, 4096, 128], P('col', 'row'), may hold values from -6 to 6
Outputs:
- output: bfloat16 [16, 4096, 128], P('col', 'row')
- grad_features: bfloat16 [16, 4096, 128], P('col', 'row')
- grad_weight1: float32 [128, 128], replicated
- grad_weight2: float32 [128, 128], replicated
The draws below stay inside these ranges and needn't reach their ends.
Inputs may be any that keep to these rules, and one draw needn't show every extreme that they name: On each device tile_coords[r, c, 0, t] is below 16 and tile_coords[r, c, 1, t] below 32; no block position appears twice among a device's 96 slots. `tile_count`: some device has all 96 slots live.
All inputs are finite; a program needn't handle non-finite values.
Results may differ from the reference program's by a relative error of at most 0.034.
Values may be sent and summed in bfloat16 or wider, within the bound.
No kernel may reach another device: no remote copies, remote signals or barrier semaphores. Data moves between devices by JAX's collectives and lax.ppermute only.
A program may use at most 64 MiB of HBM per device.

```python
import jax
import jax.numpy as jnp
from jax import lax

F = 128
BLK = 128
RB = 16
TILES_DEV = 96
ROW_SHARDS = 32
COL_SHARDS = 16
CB = 32
NODES = 65536


def draw_tile_coords(key, part):
    device_keys = jax.random.split(key, ROW_SHARDS * COL_SHARDS)

    def one_device(sub_key):
        places = jax.random.permutation(sub_key, RB * CB)[:TILES_DEV]
        return jnp.stack([places // CB, places % CB])
    coords = jax.vmap(one_device)(device_keys)
    return coords.reshape(ROW_SHARDS, COL_SHARDS, 2, TILES_DEV).astype(jnp.int32)


def draw_tile_count(key, part):
    key_shift, key_jitter, key_full = jax.random.split(key, 3)
    grid_shape = (ROW_SHARDS, COL_SHARDS)
    shifts = jax.random.randint(key_shift, grid_shape, 0, 3)
    base_count = jnp.right_shift(jnp.full(grid_shape, TILES_DEV, jnp.int32), shifts.astype(jnp.int32))
    jitter = jax.random.randint(key_jitter, grid_shape, 0, 65536).astype(jnp.int32) % (base_count // 4 + 1)
    counts = base_count - jitter
    chosen = jax.random.randint(key_full, (), 0, ROW_SHARDS * COL_SHARDS).astype(jnp.int32)
    flat_ids = jnp.arange(ROW_SHARDS * COL_SHARDS, dtype=jnp.int32).reshape(grid_shape)
    return jnp.where(flat_ids == chosen, TILES_DEV, counts).astype(jnp.int32)


def block_levels(key, shape, cuts, least, top_value):
    def one(axis_at, parts):
        draws = jax.random.uniform(jax.random.fold_in(jax.random.fold_in(key, 6), axis_at), (parts,), jnp.float32, least / len(cuts), top_value / len(cuts))
        return jnp.repeat(jnp.exp(draws), shape[axis_at] // parts).reshape((-1,) + (1,) * (len(shape) - axis_at - 1))

    loudness = one(*cuts[0])
    for cut in cuts[1:]:
        loudness = loudness * one(*cut)
    return loudness


def gaussian(key, dims, deviation, most, shards=(), held_as=jnp.bfloat16):
    level = block_levels(key, dims, shards, -0.22, 0.18) if shards else 1.0
    entries = jax.random.normal(key, dims, jnp.float32) * deviation * level
    return jnp.minimum(jnp.maximum(entries, -most), most).astype(held_as)


def setup_inputs(seed: int = 0) -> dict:
    arg_keys = jax.random.split(jax.random.key(seed), 8)
    return {
        "features": gaussian(arg_keys[0], (COL_SHARDS, CB * BLK, F), 1.0, 6.0, ((0, 16), (1, 32))),
        "weight1": gaussian(arg_keys[1], (F, F), F ** -0.5, 0.5),
        "weight2": gaussian(arg_keys[2], (F, F), F ** -0.5, 0.5),
        "tile_values": gaussian(arg_keys[3], (ROW_SHARDS, COL_SHARDS, TILES_DEV, BLK, BLK), (1.4 / (BLK * TILES_DEV * COL_SHARDS // RB) ** 0.5), 0.1875, ((0, 32), (1, 16))),
        "tile_coords": draw_tile_coords(jax.random.fold_in(arg_keys[7], 71), 0),
        "tile_count": draw_tile_count(jax.random.fold_in(arg_keys[7], 71), 0),
        "out_grad": gaussian(arg_keys[6], (COL_SHARDS, CB * BLK, F), 1.0, 6.0, ((0, 16), (1, 32))),
    }


def forward_part(tile_block, coord_block, live_count, panel_rows):
    blocks = panel_rows.reshape(CB, BLK, F)[coord_block[1]]
    products = jnp.einsum("tij,tjf->tif", tile_block.astype(jnp.float32), blocks.astype(jnp.float32))
    live_slots = jnp.arange(TILES_DEV) < live_count
    onehot = jnp.where((coord_block[0][None, :] == jnp.arange(RB)[:, None]) & live_slots[None, :], 1.0, 0.0).astype(jnp.float32)
    return jnp.einsum("rt,tif->rif", onehot, products).reshape(RB * BLK, F)


def transposed_part(tile_block, coord_block, live_count, panel_rows):
    blocks = panel_rows.reshape(RB, BLK, F)[coord_block[0]]
    products = jnp.einsum("tji,tjf->tif", tile_block.astype(jnp.float32), blocks.astype(jnp.float32))
    live_slots = jnp.arange(TILES_DEV) < live_count
    onehot = jnp.where((coord_block[1][None, :] == jnp.arange(CB)[:, None]) & live_slots[None, :], 1.0, 0.0).astype(jnp.float32)
    return jnp.einsum("ct,tif->cif", onehot, products).reshape(CB * BLK, F)


def rounded(value):
    return lax.optimization_barrier(value.astype(jnp.bfloat16)).astype(jnp.float32)


def rows_sum(tile_values, tile_coords, tile_count, col_panels):
    def per_row(row_id):
        def per_col(col_id):
            return rounded(forward_part(tile_values[row_id, col_id], tile_coords[row_id, col_id], tile_count[row_id, col_id], col_panels[col_id]))
        return jnp.sum(lax.map(per_col, jnp.arange(COL_SHARDS)), axis=0)
    return lax.map(per_row, jnp.arange(ROW_SHARDS))


def cols_sum(tile_values, tile_coords, tile_count, row_panels):
    def per_col(col_id):
        def per_row(row_id):
            return rounded(transposed_part(tile_values[row_id, col_id], tile_coords[row_id, col_id], tile_count[row_id, col_id], row_panels[row_id]))
        return jnp.sum(lax.map(per_row, jnp.arange(ROW_SHARDS)), axis=0)
    return lax.map(per_col, jnp.arange(COL_SHARDS))


def silu_slope(value):
    sigmoid = jax.nn.sigmoid(value)
    return sigmoid * (1.0 + value * (1.0 - sigmoid))


def reference(features, weight1, weight2, tile_values, tile_coords, tile_count, out_grad):
    agg_one = rows_sum(tile_values, tile_coords, tile_count, features).astype(jnp.bfloat16).reshape(NODES, F)
    pre_one = jnp.dot(agg_one, weight1, preferred_element_type=jnp.float32)
    hidden = jax.nn.silu(pre_one).astype(jnp.bfloat16)
    agg_two = cols_sum(tile_values, tile_coords, tile_count, hidden.reshape(ROW_SHARDS, RB * BLK, F)).astype(jnp.bfloat16).reshape(NODES, F)
    output = jnp.dot(agg_two, weight2, preferred_element_type=jnp.float32).astype(jnp.bfloat16)
    grad_flat = out_grad.reshape(NODES, F)
    grad_two = jnp.dot(grad_flat, weight2.T, preferred_element_type=jnp.float32).astype(jnp.bfloat16)
    grad_hidden = rows_sum(tile_values, tile_coords, tile_count, grad_two.reshape(COL_SHARDS, CB * BLK, F)).reshape(NODES, F)
    grad_pre = (grad_hidden * silu_slope(pre_one)).astype(jnp.bfloat16)
    grad_one = jnp.dot(grad_pre, weight1.T, preferred_element_type=jnp.float32).astype(jnp.bfloat16)
    grad_features = cols_sum(tile_values, tile_coords, tile_count, grad_one.reshape(ROW_SHARDS, RB * BLK, F)).astype(jnp.bfloat16)
    factor = 1.0 / (NODES ** 0.5)
    grad_weight1 = jnp.dot(agg_one.T, grad_pre, preferred_element_type=jnp.float32) * factor
    grad_weight2 = jnp.dot(agg_two.T, grad_flat, preferred_element_type=jnp.float32) * factor
    return (output.reshape(COL_SHARDS, CB * BLK, F), grad_features, grad_weight1, grad_weight2)
```

```python
import functools
import math

import jax
import jax.numpy as jnp
from jax import lax
from jax.experimental import pallas as pl
from jax.experimental.pallas import tpu as pltpu
from jax.sharding import PartitionSpec as P


def tile_kernel(transposed, coords_ref, count_ref, tiles_ref, panel_ref, out_ref, acc_ref):
    acc_ref[...] = jnp.zeros_like(acc_ref)
    source, target = (0, 1) if transposed else (1, 0)
    contract = (((0,), (0,)), ((), ())) if transposed else (((1,), (0,)), ((), ()))

    def one_slot(slot, carry):
        product = lax.dot_general(
            tiles_ref[slot],
            panel_ref[coords_ref[source, slot]],
            contract,
            preferred_element_type=jnp.float32,
        )
        acc_ref[coords_ref[target, slot]] += product
        return carry

    lax.fori_loop(0, count_ref[0], one_slot, 0)
    out_ref[...] = acc_ref[...].astype(out_ref.dtype)


def tile_products(transposed, coords, count, tiles, panel, target_blocks):
    side, width = tiles.shape[1], panel.shape[-1]
    blocks = panel.shape[0]
    vmem = pl.BlockSpec(memory_space=pltpu.VMEM)
    smem = pl.BlockSpec(memory_space=pltpu.SMEM)
    return pl.pallas_call(
        functools.partial(tile_kernel, transposed),
        out_shape=jax.ShapeDtypeStruct((target_blocks, side, width), jnp.bfloat16),
        in_specs=[smem, smem, vmem, vmem],
        out_specs=vmem,
        scratch_shapes=[pltpu.VMEM((target_blocks, side, width), jnp.float32)],
        compiler_params=pltpu.CompilerParams(vmem_limit_bytes=40 << 20),
        cost_estimate=pl.CostEstimate(
            flops=2 * tiles.shape[0] * side * side * width,
            transcendentals=0,
            bytes_accessed=2 * (tiles.size + blocks * side * width + target_blocks * side * width),
        ),
    )(coords, count, tiles, panel)


def exchange(blocks, axis):
    return lax.all_to_all(blocks, axis, 0, 0, tiled=True)


def two_halves(value):
    high = lax.reduce_precision(value, 8, 7)
    return high.astype(jnp.bfloat16), (value - high).astype(jnp.bfloat16)


def block_sum(blocks):
    return jnp.sum(blocks.astype(jnp.float32), axis=0)


def on_device(features, weight1, weight2, tile_values, tile_coords, tile_count, out_grad):
    tiles = tile_values[0, 0]
    coords = tile_coords[0, 0]
    count = tile_count[0]
    rows_n, cols_n = lax.axis_size("row"), lax.axis_size("col")
    side, feat = features.shape[1], features.shape[2]
    node_total = side * rows_n * cols_n
    f32 = functools.partial(jnp.dot, preferred_element_type=jnp.float32)
    contract = (((0,), (0,)), ((), ()))

    both = jnp.concatenate([features[0], out_grad[0]], axis=1)
    panel = exchange(jnp.broadcast_to(both[None], (rows_n, side, 2 * feat)), "row")
    parts = tile_products(False, coords, count, tiles, panel, cols_n)

    sums = block_sum(exchange(parts, "col"))
    agg_one = sums[:, :feat].astype(jnp.bfloat16)
    agg_grad = sums[:, feat:].astype(jnp.bfloat16)
    pre_one = f32(agg_one, weight1)
    sigmoid = jax.nn.sigmoid(pre_one)
    hidden = (pre_one * sigmoid).astype(jnp.bfloat16)
    grad_hidden = f32(agg_grad, weight2.T)
    grad_pre = (grad_hidden * (sigmoid * (1.0 + pre_one * (1.0 - sigmoid)))).astype(jnp.bfloat16)
    grad_one = f32(grad_pre, weight1.T).astype(jnp.bfloat16)
    term_one = lax.dot_general(agg_one, grad_pre, contract, preferred_element_type=jnp.float32)
    term_two = lax.dot_general(hidden, agg_grad, contract, preferred_element_type=jnp.float32)

    terms = jnp.concatenate([term_one, term_two], axis=1)
    slice_rows = feat // cols_n
    slices = [h.reshape(cols_n, slice_rows, 2 * feat) for h in two_halves(terms)]
    both = jnp.concatenate([hidden, grad_one], axis=1)
    sent = jnp.concatenate(
        [jnp.broadcast_to(both[None], (cols_n, side, 2 * feat)), *slices], axis=1
    )
    got = exchange(sent, "col")
    terms = block_sum(got[:, side : side + slice_rows]) + block_sum(got[:, side + slice_rows :])
    parts = tile_products(True, coords, count, tiles, got[:, :side], rows_n)

    slices = [
        jnp.broadcast_to(h[None], (rows_n, slice_rows, 2 * feat)) for h in two_halves(terms)
    ]
    got = exchange(jnp.concatenate([parts, *slices], axis=1), "row")
    sums = block_sum(got[:, :side]).astype(jnp.bfloat16)
    terms = block_sum(got[:, side : side + slice_rows]) + block_sum(got[:, side + slice_rows :])
    output = f32(sums[:, :feat], weight2).astype(jnp.bfloat16)
    grad_features = sums[:, feat:]
    weights = lax.all_gather(terms * (1.0 / math.sqrt(node_total)), "col", axis=0, tiled=True)
    return (output[None], grad_features[None], weights[:, :feat], weights[:, feat:])


def solution(mesh):
    placed = (
        P("col", "row", None),
        P(),
        P(),
        P("row", "col", None, None, None),
        P("row", "col", None, None),
        P("row", "col"),
        P("col", "row", None),
    )
    return jax.shard_map(
        on_device,
        mesh=mesh,
        in_specs=placed,
        out_specs=(P("col", "row", None), P("col", "row", None), P(), P()),
        check_vma=False,
    )
```

```python
import functools
import math

import jax
import jax.numpy as jnp
from jax import lax
from jax.experimental import pallas as pl
from jax.experimental.pallas import tpu as pltpu
from jax.sharding import Mesh, PartitionSpec as P

ROW = ("z", "yl")
COL = ("yh", "x", "c")
PLANE = ("yh", "x")
UNROLL = 16


def add_tiles(transposed, source_ref, target_ref, count_ref, tiles_ref, panel_ref, acc_ref):
    acc_ref[...] = jnp.zeros_like(acc_ref)
    spare = acc_ref.shape[0] - 1
    slots = tiles_ref.shape[0]
    unroll = math.gcd(slots, UNROLL)
    contract = (((0,), (0,)), ((), ())) if transposed else (((1,), (0,)), ((), ()))
    count = count_ref[0]

    def group(step, carry):
        for k in range(unroll):
            slot = step * unroll + k
            product = lax.dot_general(
                tiles_ref[slot],
                panel_ref[source_ref[slot]],
                contract,
                preferred_element_type=jnp.float32,
            )
            acc_ref[jnp.where(slot < count, target_ref[slot], spare)] += product
        return carry

    lax.fori_loop(0, (count + unroll - 1) // unroll, group, 0)


def forward_kernel(source_ref, target_ref, count_ref, tiles_ref, *refs):
    pieces, (keep_ref, send_ref, panel_ref, acc_ref) = refs[:-4], refs[-4:]
    n = pieces[0].shape[0]
    for i, piece in enumerate(pieces):
        panel_ref[i * n : (i + 1) * n] = piece[...]
    add_tiles(False, source_ref, target_ref, count_ref, tiles_ref, panel_ref, acc_ref)
    half = keep_ref.shape[0]
    keep_ref[...] = acc_ref[:half].astype(keep_ref.dtype)
    send_ref[...] = acc_ref[half : 2 * half].astype(send_ref.dtype)


def transposed_kernel(
    core_ref, source_ref, target_ref, count_ref, tiles_ref, mine_ref, theirs_ref, out_ref,
    panel_ref, acc_ref, term_ref,
):
    half, side = mine_ref.shape[0], tiles_ref.shape[1]
    panel_ref[:half] = mine_ref[:, :side]
    panel_ref[half:] = theirs_ref[:, :side]
    add_tiles(True, source_ref, target_ref, count_ref, tiles_ref, panel_ref, acc_ref)
    blocks = out_ref.shape[0]
    out_ref[:, :side] = acc_ref[:blocks].astype(out_ref.dtype)
    term_ref[...] = jnp.sum(mine_ref[:, side:].astype(jnp.float32), axis=0) + jnp.sum(
        theirs_ref[:, side:].astype(jnp.float32), axis=0
    )
    rows = term_ref.shape[0] // 2
    own = term_ref[pl.ds(pl.multiple_of(core_ref[0] * rows, rows), rows), :]
    out_ref[:, side:] = jnp.broadcast_to(own[None], (blocks,) + own.shape).astype(out_ref.dtype)


VMEM = pl.BlockSpec(memory_space=pltpu.VMEM)
SMEM = pl.BlockSpec(memory_space=pltpu.SMEM)
PARAMS = pltpu.CompilerParams(vmem_limit_bytes=40 << 20)


def cost(tiles, width, moved):
    return pl.CostEstimate(
        flops=2 * tiles.size * width, transcendentals=0, bytes_accessed=2 * (tiles.size + moved)
    )


def exchange(blocks, axes):
    return lax.all_to_all(blocks, axes, 0, 0, tiled=True)


def swap_cores(value):
    return lax.ppermute(value, "c", [(0, 1), (1, 0)])


def on_device(features, weight1, weight2, tile_values, tile_coords, tile_count, out_grad):
    tiles = tile_values[0, 0]
    block_rows, block_cols = tile_coords[0, 0, 0], tile_coords[0, 0, 1]
    count = tile_count[0]
    side, feat = features.shape[1], features.shape[2]
    z_n, yl_n = lax.axis_size("z"), lax.axis_size("yl")
    rows_n, cols_n = z_n * yl_n, lax.axis_size(COL)
    plane_n = cols_n // 2
    core = lax.axis_index("c").astype(jnp.int32)
    z = lax.axis_index("z").astype(jnp.int32)
    width = 2 * feat
    node_total = side * rows_n * cols_n
    dot = functools.partial(jnp.dot, preferred_element_type=jnp.float32)
    contract = (((0,), (0,)), ((), ()))

    both = jnp.concatenate([features[0], out_grad[0]], axis=1)
    own = lax.all_gather(both, "yl", axis=0, tiled=True).reshape(yl_n, side, width)
    up = [(i, (i + 1) % z_n) for i in range(z_n)]
    down = [(i, (i - 1) % z_n) for i in range(z_n)]
    behind, ahead = [own], [own]
    for step in range(z_n // 2):
        behind.append(lax.ppermute(behind[-1], "z", up))
        if step < z_n // 2 - 1:
            ahead.append(lax.ppermute(ahead[-1], "z", down))
    pieces = ahead + behind[:0:-1]

    source = ((block_cols // yl_n - z) % z_n) * yl_n + block_cols % yl_n
    row_place = ((block_rows % 2) ^ core) * plane_n + block_rows // 2
    half = jax.ShapeDtypeStruct((plane_n, side, width), jnp.bfloat16)
    keep, send = pl.pallas_call(
        forward_kernel,
        out_shape=(half, half),
        in_specs=[SMEM] * 3 + [VMEM] * (1 + len(pieces)),
        out_specs=(VMEM, VMEM),
        scratch_shapes=[
            pltpu.VMEM((rows_n, side, width), jnp.bfloat16),
            pltpu.VMEM((cols_n + 1, side, width), jnp.float32),
        ],
        compiler_params=PARAMS,
        cost_estimate=cost(tiles, width, (rows_n + cols_n) * side * width),
    )(source, row_place, count, tiles, *pieces)

    pair = keep.astype(jnp.float32) + swap_cores(send).astype(jnp.float32)
    got = exchange(pair.astype(jnp.bfloat16), PLANE)
    sums = jnp.sum(got.astype(jnp.float32), axis=0)
    agg_one = sums[:, :feat].astype(jnp.bfloat16)
    agg_grad = sums[:, feat:].astype(jnp.bfloat16)
    pre_one = dot(agg_one, weight1)
    sigmoid = jax.nn.sigmoid(pre_one)
    hidden = (pre_one * sigmoid).astype(jnp.bfloat16)
    grad_hidden = dot(agg_grad, weight2.T)
    grad_pre = (grad_hidden * (sigmoid * (1.0 + pre_one * (1.0 - sigmoid)))).astype(jnp.bfloat16)
    grad_one = dot(grad_pre, weight1.T).astype(jnp.bfloat16)
    term_one = lax.dot_general(agg_one, grad_pre, contract, preferred_element_type=jnp.float32)
    term_two = lax.dot_general(hidden, agg_grad, contract, preferred_element_type=jnp.float32)

    both = jnp.concatenate([hidden, grad_one], axis=1)
    slices = jnp.concatenate([term_one, term_two], axis=1).astype(jnp.bfloat16)
    slices = slices.reshape(plane_n, feat // plane_n, width)
    sent = jnp.concatenate(
        [jnp.broadcast_to(both[None], (plane_n, side, width)), slices], axis=1
    )
    mine = exchange(sent, PLANE)
    theirs = swap_cores(mine)
    slice_rows = feat // cols_n
    parts = pl.pallas_call(
        transposed_kernel,
        out_shape=jax.ShapeDtypeStruct((rows_n, side + slice_rows, width), jnp.bfloat16),
        in_specs=[SMEM] * 4 + [VMEM] * 3,
        out_specs=VMEM,
        scratch_shapes=[
            pltpu.VMEM((cols_n, side, width), jnp.bfloat16),
            pltpu.VMEM((rows_n + 1, side, width), jnp.float32),
            pltpu.VMEM((2 * slice_rows, width), jnp.float32),
        ],
        compiler_params=PARAMS,
        cost_estimate=cost(tiles, width, (rows_n + cols_n) * side * width),
    )(core.reshape(1), row_place, block_cols, count, tiles, mine, theirs)

    got = exchange(parts, ROW)
    sums = jnp.sum(got[:, :side].astype(jnp.float32), axis=0).astype(jnp.bfloat16)
    terms = jnp.sum(got[:, side:].astype(jnp.float32), axis=0)
    output = dot(sums[:, :feat], weight2).astype(jnp.bfloat16)
    grad_features = sums[:, feat:]
    terms = terms * (1.0 / math.sqrt(node_total))
    weights = exchange(jnp.broadcast_to(terms[None], (cols_n,) + terms.shape), COL)
    weights = weights.reshape(feat, width)
    return (output[None], grad_features[None], weights[:, :feat], weights[:, feat:])


def solution(mesh):
    fine = Mesh(mesh.devices.reshape(8, 4, 2, 4, 2), ("z", "yl", "yh", "x", "c"))
    placed = (
        P(COL, ROW, None),
        P(),
        P(),
        P(ROW, COL, None, None, None),
        P(ROW, COL, None, None),
        P(ROW, COL),
        P(COL, ROW, None),
    )
    return jax.shard_map(
        on_device,
        mesh=fine,
        in_specs=placed,
        out_specs=(P(COL, ROW, None), P(COL, ROW, None), P(), P()),
        check_vma=False,
    )
```

```python
import functools
import math

import jax
import jax.numpy as jnp
from jax import lax
from jax.experimental import pallas as pl
from jax.experimental.pallas import tpu as pltpu
from jax.sharding import Mesh, PartitionSpec as P

ROW = ("z", "yl")
COL = ("yh", "x", "c")
SLICES = ("x", "yh", "c")
UNROLL = 16


def add_tiles(transposed, first, count, source_ref, target_ref, tiles_ref, panel_ref, acc_ref):
    spare = acc_ref.shape[0] - 1
    contract = (((0,), (0,)), ((), ())) if transposed else (((1,), (0,)), ((), ()))
    for k in range(tiles_ref.shape[0]):
        slot = first + k
        product = lax.dot_general(
            tiles_ref[k],
            panel_ref[source_ref[slot]],
            contract,
            preferred_element_type=jnp.float32,
        )
        acc_ref[jnp.where(slot < count, target_ref[slot], spare)] += product


def forward_kernel(source_ref, target_ref, count_ref, tiles_ref, *refs):
    pieces, (keep_ref, send_ref, held_ref, panel_ref, acc_ref, sems) = refs[:-6], refs[-6:]
    steps = sems.shape[0]
    group = held_ref.shape[0] // steps
    copies = [
        pltpu.make_async_copy(
            tiles_ref.at[pl.ds(i * group, group)], held_ref.at[pl.ds(i * group, group)], sems.at[i]
        )
        for i in range(steps)
    ]
    for copy in copies:
        copy.start()
    acc_ref[...] = jnp.zeros_like(acc_ref)
    n = pieces[0].shape[0]
    for i, piece in enumerate(pieces):
        panel_ref[i * n : (i + 1) * n] = piece[...]
    count = count_ref[0]
    for i, copy in enumerate(copies):
        copy.wait()

        @pl.when(i * group < count)
        def _():
            tiles = held_ref.at[pl.ds(i * group, group)]
            add_tiles(False, i * group, count, source_ref, target_ref, tiles, panel_ref, acc_ref)

    half = keep_ref.shape[0]
    keep_ref[...] = acc_ref[:half].astype(keep_ref.dtype)
    send_ref[...] = acc_ref[half : 2 * half].astype(send_ref.dtype)


def transposed_kernel(
    part_ref, source_ref, target_ref, count_ref, tiles_ref, mine_ref, theirs_ref,
    out_ref, terms_ref, panel_ref, acc_ref, sum_ref, rounded_ref, sems,
):
    side = tiles_ref.shape[1]
    acc_ref[...] = jnp.zeros_like(acc_ref)
    places = mine_ref.shape[0]
    held = panel_ref.shape[0] // (2 * places)
    for i, ref in enumerate((mine_ref, theirs_ref)):
        for k in range(held):
            for place in range(places):
                panel_ref[(i * places + place) * held + k] = ref[place, k * side : (k + 1) * side]
    rest = held * side
    sum_ref[...] = jnp.sum(mine_ref[:, rest:].astype(jnp.float32), axis=0) + jnp.sum(
        theirs_ref[:, rest:].astype(jnp.float32), axis=0
    )
    rows = terms_ref.shape[1]
    own = sum_ref[pl.ds(pl.multiple_of(part_ref[0] * rows, rows), rows), :]
    terms_ref[...] = jnp.broadcast_to(own[None], terms_ref.shape)

    count = count_ref[0]
    slots = tiles_ref.shape[0]
    group = math.gcd(slots, UNROLL)
    for first in range(0, slots, group):

        @pl.when(first < count)
        def _():
            tiles = tiles_ref.at[pl.ds(first, group)]
            add_tiles(True, first, count, source_ref, target_ref, tiles, panel_ref, acc_ref)

    steps = sems.shape[0]
    blocks = rounded_ref.shape[0] // steps
    copies = []
    for i in range(steps):
        window = pl.ds(i * blocks, blocks)
        rounded_ref[window] = acc_ref[window].astype(rounded_ref.dtype)
        copies.append(
            pltpu.make_async_copy(rounded_ref.at[window], out_ref.at[window], sems.at[i])
        )
        copies[-1].start()
    for copy in copies:
        copy.wait()


VMEM = pl.BlockSpec(memory_space=pltpu.VMEM)
SMEM = pl.BlockSpec(memory_space=pltpu.SMEM)
HBM = pl.BlockSpec(memory_space=pltpu.HBM)
PARAMS = pltpu.CompilerParams(vmem_limit_bytes=40 << 20)


def cost(tiles, width, moved):
    return pl.CostEstimate(
        flops=2 * tiles.size * width, transcendentals=0, bytes_accessed=2 * (tiles.size + moved)
    )


def exchange(blocks, axes):
    return lax.all_to_all(blocks, axes, 0, 0, tiled=True)


def swap_cores(value):
    return lax.ppermute(value, "c", [(0, 1), (1, 0)])


def on_device(features, weight1, weight2, tile_values, tile_coords, tile_count, out_grad):
    tiles = tile_values[0, 0]
    block_rows, block_cols = tile_coords[0, 0, 0], tile_coords[0, 0, 1]
    count = tile_count[0]
    side, feat = features.shape[1], features.shape[2]
    z_n, yl_n = lax.axis_size("z"), lax.axis_size("yl")
    rows_n, cols_n = z_n * yl_n, lax.axis_size(COL)
    x_n, yh_n = lax.axis_size("x"), lax.axis_size("yh")
    half_n = cols_n // 2
    core = lax.axis_index("c").astype(jnp.int32)
    z = lax.axis_index("z").astype(jnp.int32)
    width = 2 * feat
    node_total = side * rows_n * cols_n
    dot = functools.partial(jnp.dot, preferred_element_type=jnp.float32)
    contract = (((0,), (0,)), ((), ()))

    both = jnp.concatenate([features[0], out_grad[0]], axis=1)
    own = lax.all_gather(both, "yl", axis=0, tiled=True).reshape(yl_n, side, width)
    up = [(i, (i + 1) % z_n) for i in range(z_n)]
    down = [(i, (i - 1) % z_n) for i in range(z_n)]
    behind, ahead = [own], [own]
    for step in range(z_n // 2):
        behind.append(lax.ppermute(behind[-1], "z", up))
        if step < z_n // 2 - 1:
            ahead.append(lax.ppermute(ahead[-1], "z", down))
    pieces = ahead + behind[:0:-1]

    source = ((block_cols // yl_n - z) % z_n) * yl_n + block_cols % yl_n
    row_place = (
        ((block_rows % 2) ^ core) * half_n
        + (block_rows // 2 % x_n) * yh_n
        + block_rows // (2 * x_n)
    )
    half = jax.ShapeDtypeStruct((half_n, side, width), jnp.bfloat16)
    keep, send = pl.pallas_call(
        forward_kernel,
        out_shape=(half, half),
        in_specs=[SMEM] * 3 + [HBM] + [VMEM] * len(pieces),
        out_specs=(VMEM, VMEM),
        scratch_shapes=[
            pltpu.VMEM(tiles.shape, jnp.bfloat16),
            pltpu.VMEM((rows_n, side, width), jnp.bfloat16),
            pltpu.VMEM((cols_n + 1, side, width), jnp.float32),
            pltpu.SemaphoreType.DMA((tiles.shape[0] // math.gcd(tiles.shape[0], UNROLL),)),
        ],
        compiler_params=PARAMS,
        cost_estimate=cost(tiles, width, (rows_n + cols_n) * side * width),
    )(source, row_place, count, pltpu.with_memory_space_constraint(tiles, pltpu.HBM), *pieces)

    pair = keep.astype(jnp.float32) + swap_cores(send).astype(jnp.float32)
    got = exchange(pair.astype(jnp.bfloat16), "x").reshape(x_n, yh_n * side, width)
    sums = jnp.sum(got.astype(jnp.float32), axis=0).astype(jnp.bfloat16)
    swapped = lax.ppermute(sums, "yh", [(0, 1), (1, 0)])
    sums = sums.astype(jnp.float32) + swapped.astype(jnp.float32)
    agg_one = sums[:, :feat].astype(jnp.bfloat16)
    agg_grad = sums[:, feat:].astype(jnp.bfloat16)
    pre_one = dot(agg_one, weight1)
    sigmoid = jax.nn.sigmoid(pre_one)
    hidden = (pre_one * sigmoid).astype(jnp.bfloat16)
    grad_hidden = dot(agg_grad, weight2.T)
    grad_pre = (grad_hidden * (sigmoid * (1.0 + pre_one * (1.0 - sigmoid)))).astype(jnp.bfloat16)
    grad_one = dot(grad_pre, weight1.T).astype(jnp.bfloat16)
    term_one = lax.dot_general(agg_one, grad_pre, contract, preferred_element_type=jnp.float32)
    term_two = lax.dot_general(hidden, agg_grad, contract, preferred_element_type=jnp.float32)

    both = jnp.concatenate([hidden, grad_one], axis=1)
    slices = jnp.concatenate([term_one, term_two], axis=1).astype(jnp.bfloat16)
    slices = slices.reshape(x_n, feat // x_n, width)
    sent = jnp.concatenate(
        [jnp.broadcast_to(both[None], (x_n,) + both.shape), slices], axis=1
    )
    mine = exchange(sent, "x")
    theirs = swap_cores(mine)
    part = lax.axis_index("yh").astype(jnp.int32) * 2 + core
    parts, terms = pl.pallas_call(
        transposed_kernel,
        out_shape=(
            pltpu.HBM((rows_n, side, width), jnp.bfloat16),
            jax.ShapeDtypeStruct((rows_n, feat // cols_n, width), jnp.float32),
        ),
        in_specs=[SMEM] * 4 + [VMEM] * 3,
        out_specs=(HBM, VMEM),
        scratch_shapes=[
            pltpu.VMEM((cols_n, side, width), jnp.bfloat16),
            pltpu.VMEM((rows_n + 1, side, width), jnp.float32),
            pltpu.VMEM((feat // x_n, width), jnp.float32),
            pltpu.VMEM((rows_n, side, width), jnp.bfloat16),
            pltpu.SemaphoreType.DMA((z_n,)),
        ],
        compiler_params=PARAMS,
        cost_estimate=cost(tiles, width, (rows_n + cols_n) * side * width),
    )(part.reshape(1), row_place, block_cols, count, tiles, mine, theirs)

    sums = lax.psum_scatter(parts, "z", scatter_dimension=0, tiled=True)
    terms = jnp.sum(exchange(terms, ROW), axis=0) * (1.0 / math.sqrt(node_total))
    weights = exchange(jnp.broadcast_to(terms[None], (cols_n,) + terms.shape), SLICES)
    sums = jnp.sum(exchange(sums, "yl").astype(jnp.float32), axis=0).astype(jnp.bfloat16)
    output = dot(sums[:, :feat], weight2).astype(jnp.bfloat16)
    grad_features = sums[:, feat:]
    weights = weights.reshape(feat, width)
    return (output[None], grad_features[None], weights[:, :feat], weights[:, feat:])


def solution(mesh):
    fine = Mesh(mesh.devices.reshape(8, 4, 2, 4, 2), ("z", "yl", "yh", "x", "c"))
    placed = (
        P(COL, ROW, None),
        P(),
        P(),
        P(ROW, COL, None, None, None),
        P(ROW, COL, None, None),
        P(ROW, COL),
        P(COL, ROW, None),
    )
    return jax.shard_map(
        on_device,
        mesh=fine,
        in_specs=placed,
        out_specs=(P(COL, ROW, None), P(COL, ROW, None), P(), P()),
        check_vma=False,
    )
```

```python
import functools
import math

import jax
import jax.numpy as jnp
from jax import lax
from jax.experimental import pallas as pl
from jax.experimental.pallas import tpu as pltpu
from jax.sharding import Mesh, PartitionSpec as P

ROW = ("z", "yl")
COL = ("yh", "x", "c")
UNROLL = 16


def add_tiles(transposed, first, count, source_ref, target_ref, tiles_ref, panel_ref, acc_ref):
    spare = acc_ref.shape[0] - 1
    contract = (((0,), (0,)), ((), ())) if transposed else (((1,), (0,)), ((), ()))
    for k in range(tiles_ref.shape[0]):
        slot = first + k
        product = lax.dot_general(
            tiles_ref[k],
            panel_ref[source_ref[slot]],
            contract,
            preferred_element_type=jnp.float32,
        )
        acc_ref[jnp.where(slot < count, target_ref[slot], spare)] += product


def forward_kernel(source_ref, target_ref, count_ref, tiles_ref, *refs):
    pieces, (keep_ref, send_ref, held_ref, panel_ref, acc_ref, sems) = refs[:-6], refs[-6:]
    steps = sems.shape[0]
    group = held_ref.shape[0] // steps
    copies = [
        pltpu.make_async_copy(
            tiles_ref.at[pl.ds(i * group, group)], held_ref.at[pl.ds(i * group, group)], sems.at[i]
        )
        for i in range(steps)
    ]
    for copy in copies:
        copy.start()
    acc_ref[...] = jnp.zeros_like(acc_ref)
    n = pieces[0].shape[0]
    for i, piece in enumerate(pieces):
        panel_ref[i * n : (i + 1) * n] = piece[...]
    count = count_ref[0]
    for i, copy in enumerate(copies):
        copy.wait()

        @pl.when(i * group < count)
        def _():
            tiles = held_ref.at[pl.ds(i * group, group)]
            add_tiles(False, i * group, count, source_ref, target_ref, tiles, panel_ref, acc_ref)

    half = keep_ref.shape[0]
    keep_ref[...] = acc_ref[:half].astype(keep_ref.dtype)
    send_ref[...] = acc_ref[half : 2 * half].astype(send_ref.dtype)


def transposed_kernel(
    source_ref, target_ref, count_ref, tiles_ref, mine_ref, theirs_ref, *refs
):
    outs, (term_ref, panel_ref, acc_ref) = refs[:-3], refs[-3:]
    side = tiles_ref.shape[1]
    acc_ref[...] = jnp.zeros_like(acc_ref)
    places = mine_ref.shape[0]
    held = panel_ref.shape[0] // (2 * places)
    for i, ref in enumerate((mine_ref, theirs_ref)):
        for k in range(held):
            for place in range(places):
                panel_ref[(i * places + place) * held + k] = ref[place, k * side : (k + 1) * side]
    rest = held * side
    terms = jnp.sum(mine_ref[:, rest:].astype(jnp.float32), axis=0) + jnp.sum(
        theirs_ref[:, rest:].astype(jnp.float32), axis=0
    )
    term_ref[...] = terms.astype(term_ref.dtype)

    count = count_ref[0]
    slots = tiles_ref.shape[0]
    group = math.gcd(slots, UNROLL)
    for first in range(0, slots, group):

        @pl.when(first < count)
        def _():
            tiles = tiles_ref.at[pl.ds(first, group)]
            add_tiles(True, first, count, source_ref, target_ref, tiles, panel_ref, acc_ref)

    blocks = (acc_ref.shape[0] - 1) // len(outs)
    rest = blocks * side
    firsts = (len(outs) // 2 - 1, len(outs) // 2)
    for k, out_ref in enumerate(outs):
        for i in range(blocks):
            out_ref[i * side : (i + 1) * side] = acc_ref[k * blocks + i].astype(out_ref.dtype)
        if k in firsts:
            out_ref[rest:] = term_ref[...]
        elif k:
            out_ref[rest:] = jnp.zeros_like(term_ref)


def ring_sum_kernel(z_ref, own_ref, term_ref, *refs):
    got, (out_ref, held_ref) = refs[:-2], refs[-2:]
    blocks, side = out_ref.shape[0], own_ref.shape[0] // out_ref.shape[0]
    places = len(got) + 1
    rest = own_ref.shape[0]
    held_ref[z_ref[0]] = term_ref[...]
    for k, ref in enumerate(got):
        held_ref[lax.rem(z_ref[0] + k + 1, places)] = ref[rest:]
    terms = jnp.sum(held_ref[...].astype(jnp.float32), axis=0).astype(out_ref.dtype)
    ahead, behind = got[places // 2 - 1], got[places // 2]
    for i in range(blocks):
        rows = pl.ds(i * side, side)
        total = own_ref[rows].astype(jnp.float32) + ahead[rows].astype(jnp.float32)
        out_ref[i, :side] = (total + behind[rows].astype(jnp.float32)).astype(out_ref.dtype)
        out_ref[i, side:] = terms


VMEM = pl.BlockSpec(memory_space=pltpu.VMEM)
SMEM = pl.BlockSpec(memory_space=pltpu.SMEM)
HBM = pl.BlockSpec(memory_space=pltpu.HBM)
PARAMS = pltpu.CompilerParams(vmem_limit_bytes=40 << 20)


def cost(tiles, width, moved):
    return pl.CostEstimate(
        flops=2 * tiles.size * width, transcendentals=0, bytes_accessed=2 * (tiles.size + moved)
    )


def exchange(blocks, axes):
    return lax.all_to_all(blocks, axes, 0, 0, tiled=True)


def add(left, right):
    return (left.astype(jnp.float32) + right.astype(jnp.float32)).astype(jnp.bfloat16)


def swap_cores(value):
    return lax.ppermute(value, "c", [(0, 1), (1, 0)])


def on_device(features, weight1, weight2, tile_values, tile_coords, tile_count, out_grad):
    tiles = tile_values[0, 0]
    block_rows, block_cols = tile_coords[0, 0, 0], tile_coords[0, 0, 1]
    count = tile_count[0]
    side, feat = features.shape[1], features.shape[2]
    z_n, yl_n = lax.axis_size("z"), lax.axis_size("yl")
    rows_n, cols_n = z_n * yl_n, lax.axis_size(COL)
    x_n, yh_n = lax.axis_size("x"), lax.axis_size("yh")
    half_n = cols_n // 2
    core = lax.axis_index("c").astype(jnp.int32)
    z = lax.axis_index("z").astype(jnp.int32)
    width = 2 * feat
    node_total = side * rows_n * cols_n
    dot = functools.partial(jnp.dot, preferred_element_type=jnp.float32)
    contract = (((0,), (0,)), ((), ()))

    both = jnp.concatenate([features[0], out_grad[0]], axis=1)
    own = lax.all_gather(both, "yl", axis=0, tiled=True).reshape(yl_n, side, width)
    up = [(i, (i + 1) % z_n) for i in range(z_n)]
    down = [(i, (i - 1) % z_n) for i in range(z_n)]
    behind, ahead = [own], [own]
    for step in range(z_n // 2):
        behind.append(lax.ppermute(behind[-1], "z", up))
        if step < z_n // 2 - 1:
            ahead.append(lax.ppermute(ahead[-1], "z", down))
    pieces = ahead + behind[:0:-1]

    source = ((block_cols // yl_n - z) % z_n) * yl_n + block_cols % yl_n
    row_place = (
        ((block_rows % 2) ^ core) * half_n
        + (block_rows // 2 % x_n) * yh_n
        + block_rows // (2 * x_n)
    )
    half = jax.ShapeDtypeStruct((half_n, side, width), jnp.bfloat16)
    keep, send = pl.pallas_call(
        forward_kernel,
        out_shape=(half, half),
        in_specs=[SMEM] * 3 + [HBM] + [VMEM] * len(pieces),
        out_specs=(VMEM, VMEM),
        scratch_shapes=[
            pltpu.VMEM(tiles.shape, jnp.bfloat16),
            pltpu.VMEM((rows_n, side, width), jnp.bfloat16),
            pltpu.VMEM((cols_n + 1, side, width), jnp.float32),
            pltpu.SemaphoreType.DMA((tiles.shape[0] // math.gcd(tiles.shape[0], UNROLL),)),
        ],
        compiler_params=PARAMS,
        cost_estimate=cost(tiles, width, (rows_n + cols_n) * side * width),
    )(source, row_place, count, pltpu.with_memory_space_constraint(tiles, pltpu.HBM), *pieces)

    pair = keep.astype(jnp.float32) + swap_cores(send).astype(jnp.float32)
    got = exchange(pair.astype(jnp.bfloat16), "x").reshape(x_n, yh_n * side, width)
    sums = jnp.sum(got.astype(jnp.float32), axis=0).astype(jnp.bfloat16)
    swapped = lax.ppermute(sums, "yh", [(0, 1), (1, 0)])
    sums = sums.astype(jnp.float32) + swapped.astype(jnp.float32)
    agg_one = sums[:, :feat].astype(jnp.bfloat16)
    agg_grad = sums[:, feat:].astype(jnp.bfloat16)
    pre_one = dot(agg_one, weight1)
    sigmoid = jax.nn.sigmoid(pre_one)
    hidden = (pre_one * sigmoid).astype(jnp.bfloat16)
    grad_hidden = dot(agg_grad, weight2.T)
    grad_pre = (grad_hidden * (sigmoid * (1.0 + pre_one * (1.0 - sigmoid)))).astype(jnp.bfloat16)
    grad_one = dot(grad_pre, weight1.T).astype(jnp.bfloat16)
    term_one = lax.dot_general(agg_one, grad_pre, contract, preferred_element_type=jnp.float32)
    term_two = lax.dot_general(hidden, agg_grad, contract, preferred_element_type=jnp.float32)

    both = jnp.concatenate([hidden, grad_one], axis=1)
    slices = jnp.concatenate([term_one, term_two], axis=1).astype(jnp.bfloat16)
    slices = slices.reshape(x_n, feat // x_n, width)
    sent = jnp.concatenate(
        [jnp.broadcast_to(both[None], (x_n,) + both.shape), slices], axis=1
    )
    mine = exchange(sent, "x")
    theirs = swap_cores(mine)
    term_rows = feat // x_n
    message = jax.ShapeDtypeStruct((yl_n * side + term_rows, width), jnp.bfloat16)
    *chunks, terms = pl.pallas_call(
        transposed_kernel,
        out_shape=(
            jax.ShapeDtypeStruct((yl_n * side, width), jnp.bfloat16),
            *[message] * (z_n - 1),
            jax.ShapeDtypeStruct((term_rows, width), jnp.bfloat16),
        ),
        in_specs=[SMEM] * 3 + [VMEM] * 3,
        out_specs=(VMEM,) * (z_n + 1),
        scratch_shapes=[
            pltpu.VMEM((cols_n, side, width), jnp.bfloat16),
            pltpu.VMEM((rows_n + 1, side, width), jnp.float32),
        ],
        compiler_params=PARAMS,
        cost_estimate=cost(tiles, width, (rows_n + cols_n) * side * width),
    )(row_place, source, count, tiles, mine, theirs)

    middle = z_n // 2
    ahead, behind = [], []
    down_sum, up_sum = chunks[middle], chunks[middle - 1]
    for step in range(middle):
        ahead.append(lax.ppermute(down_sum, "z", down))
        if step < middle - 1:
            behind.append(lax.ppermute(up_sum, "z", up))
            down_sum = add(ahead[-1], chunks[middle + 1 + step])
        if step < middle - 2:
            up_sum = add(behind[-1], chunks[middle - 2 - step])
    sent = pl.pallas_call(
        ring_sum_kernel,
        out_shape=jax.ShapeDtypeStruct((yl_n, side + term_rows, width), jnp.bfloat16),
        in_specs=[SMEM] + [VMEM] * (z_n + 1),
        out_specs=VMEM,
        scratch_shapes=[pltpu.VMEM((z_n, term_rows, width), jnp.bfloat16)],
        compiler_params=PARAMS,
    )(z.reshape(1), chunks[0], terms, *ahead, *behind[::-1])
    got = exchange(sent, "yl")
    terms = jnp.sum(got[:, side:].astype(jnp.float32), axis=0) * (1.0 / math.sqrt(node_total))
    weights = exchange(jnp.broadcast_to(terms[None], (x_n,) + terms.shape), "x")
    sums = jnp.sum(got[:, :side].astype(jnp.float32), axis=0).astype(jnp.bfloat16)
    output = dot(sums[:, :feat], weight2).astype(jnp.bfloat16)
    grad_features = sums[:, feat:]
    weights = weights.reshape(feat, width)
    return (output[None], grad_features[None], weights[:, :feat], weights[:, feat:])


def solution(mesh):
    fine = Mesh(mesh.devices.reshape(8, 4, 2, 4, 2), ("z", "yl", "yh", "x", "c"))
    placed = (
        P(COL, ROW, None),
        P(),
        P(),
        P(ROW, COL, None, None, None),
        P(ROW, COL, None, None),
        P(ROW, COL),
        P(COL, ROW, None),
    )
    return jax.shard_map(
        on_device,
        mesh=fine,
        in_specs=placed,
        out_specs=(P(COL, ROW, None), P(COL, ROW, None), P(), P()),
        check_vma=False,
    )
```

```python
import functools
import math

import jax
import jax.numpy as jnp
from jax import lax
from jax.experimental import pallas as pl
from jax.experimental.pallas import tpu as pltpu
from jax.sharding import Mesh, PartitionSpec as P

ROW = ("z", "yl")
COL = ("yh", "x", "c")
UNROLL = 16
MINE, FIRST, REST = range(3)


def add_slots(first, count, source_ref, target_ref, tiles_ref, panel_ref, acc_ref):
    spare = acc_ref.shape[0] - 1
    for k in range(tiles_ref.shape[0]):
        slot = first + k
        product = jnp.dot(
            tiles_ref[k], panel_ref[source_ref[slot]], preferred_element_type=jnp.float32
        )
        acc_ref[jnp.where(slot < count, target_ref[slot], spare)] += product


def forward_kernel(source_ref, target_ref, count_ref, tiles_ref, *refs):
    pieces, (keep_ref, send_ref, held_ref, panel_ref, acc_ref, sems) = refs[:-6], refs[-6:]
    steps = sems.shape[0]
    group = held_ref.shape[0] // steps
    copies = [
        pltpu.make_async_copy(
            tiles_ref.at[pl.ds(i * group, group)], held_ref.at[pl.ds(i * group, group)], sems.at[i]
        )
        for i in range(steps)
    ]
    for copy in copies:
        copy.start()
    acc_ref[...] = jnp.zeros_like(acc_ref)
    n = pieces[0].shape[0]
    for i, piece in enumerate(pieces):
        panel_ref[i * n : (i + 1) * n] = piece[...]
    count = count_ref[0]
    for i, copy in enumerate(copies):
        copy.wait()

        @pl.when(i * group < count)
        def _():
            tiles = held_ref.at[pl.ds(i * group, group)]
            add_slots(i * group, count, source_ref, target_ref, tiles, panel_ref, acc_ref)

    half = keep_ref.shape[0]
    keep_ref[...] = acc_ref[:half].astype(keep_ref.dtype)
    send_ref[...] = acc_ref[half : 2 * half].astype(send_ref.dtype)


def shift(value, n):
    return lax.shift_right_logical(value, jnp.int32(n.bit_length() - 1))


def plan_kernel(sizes, coords_ref, count_ref, list_ref, size_ref):
    z_n, yl_n, yh_n, x_n = sizes
    middle = z_n // 2
    slots, groups = coords_ref.shape[0], size_ref.shape[0]
    unroll = math.gcd(slots, 4)
    z, core, count = (coords_ref[0] >> 16) & 255, coords_ref[0] >> 24, count_ref[0]

    def step(first, ends):
        ends = list(ends)
        for k in range(unroll):
            slot = first * unroll + k
            row, col = coords_ref[slot] & 255, (coords_ref[slot] >> 8) & 255
            turn = (shift(col, yl_n) - z) & (z_n - 1)
            place = (shift(row, 2) & (x_n - 1)) * yh_n + shift(row, 2 * x_n)
            block = turn * yl_n + (col & (yl_n - 1))
            mine = (row & 1) == core
            chunks = (turn == middle) | (turn == middle - 1)
            group = jnp.where(mine, MINE, jnp.where(chunks, FIRST, REST))
            target = jnp.where(~mine & chunks, block - (middle - 1) * yl_n, block)
            at = jnp.int32(groups * slots)
            for g in range(groups):
                chosen = (slot < count) & (group == g)
                at = jnp.where(chosen, g * slots + ends[g], at)
                ends[g] = ends[g] + chosen.astype(jnp.int32)
            list_ref[at] = slot + (place << 8) + (target << 16)
        return tuple(ends)

    ends = lax.fori_loop(0, (count + unroll - 1) // unroll, step, (jnp.int32(0),) * groups)
    for group in range(groups):
        size_ref[group] = ends[group]


def add_tiles(unroll, group, list_ref, size_ref, tiles_ref, read, acc_ref):
    spare, slots = acc_ref.shape[0] - 1, tiles_ref.shape[0]
    contract = (((0,), (0,)), ((), ()))
    size = size_ref[group]

    def step(first, carry):
        for k in range(unroll):
            at = first * unroll + k
            live = at < size
            entry = list_ref[slots * group + jnp.minimum(at, slots - 1)]
            entry = jnp.where(live, entry, spare << 16)
            slot, source, target = entry & 255, (entry >> 8) & 255, entry >> 16
            product = lax.dot_general(
                tiles_ref[slot], read(source), contract, preferred_element_type=jnp.float32
            )
            acc_ref[target] += product
        return carry

    lax.fori_loop(0, (size + unroll - 1) // unroll, step, 0)


def reader(ref, side, held):
    def read(source):
        start = pl.multiple_of(lax.rem(source, held) * side, side)
        return ref[source // held, pl.ds(start, side), :]

    return read


def mine_kernel(held, list_ref, size_ref, tiles_ref, mine_ref, acc_ref):
    acc_ref[...] = jnp.zeros_like(acc_ref)
    read = reader(mine_ref, tiles_ref.shape[1], held)
    add_tiles(16, MINE, list_ref, size_ref, tiles_ref, read, acc_ref)


def first_kernel(
    held, begin, list_ref, size_ref, tiles_ref, mine_ref, theirs_ref, begun_ref,
    up_ref, down_ref, term_ref, acc_ref,
):
    side = tiles_ref.shape[1]
    blocks = acc_ref.shape[0] - 1
    acc_ref[:blocks] = begun_ref[begin : begin + blocks]
    acc_ref[blocks] = jnp.zeros_like(acc_ref[blocks])
    read = reader(theirs_ref, side, held)
    add_tiles(8, FIRST, list_ref, size_ref, tiles_ref, read, acc_ref)
    terms = jnp.sum(mine_ref[:, held * side :].astype(jnp.float32), axis=0) + jnp.sum(
        theirs_ref[:, held * side :].astype(jnp.float32), axis=0
    )
    terms = terms.astype(term_ref.dtype)
    term_ref[...] = terms
    for i in range(blocks // 2):
        rows = pl.ds(i * side, side)
        up_ref[rows] = acc_ref[i].astype(up_ref.dtype)
        down_ref[rows] = acc_ref[blocks // 2 + i].astype(down_ref.dtype)
    rest = blocks // 2 * side
    up_ref[rest:] = terms
    down_ref[rest:] = terms


def rest_kernel(held, turns, list_ref, size_ref, tiles_ref, theirs_ref, begun_ref, *refs):
    outs, acc_ref = refs[:-1], refs[-1]
    side = tiles_ref.shape[1]
    n = outs[0].shape[0] // side
    spare = acc_ref.shape[0] - 1
    acc_ref[spare] = jnp.zeros_like(acc_ref[spare])
    for turn in turns:
        acc_ref[turn * n : (turn + 1) * n] = begun_ref[turn * n : (turn + 1) * n]
    read = reader(theirs_ref, side, held)
    add_tiles(16, REST, list_ref, size_ref, tiles_ref, read, acc_ref)
    for turn, out_ref in zip(turns, outs):
        for i in range(n):
            out_ref[i * side : (i + 1) * side] = acc_ref[turn * n + i].astype(out_ref.dtype)
        if turn:
            out_ref[n * side :] = jnp.zeros_like(out_ref[n * side :])


def ring_sum_kernel(coords_ref, own_ref, term_ref, *refs):
    got, (out_ref, held_ref) = refs[:-2], refs[-2:]
    blocks, side = out_ref.shape[0], own_ref.shape[0] // out_ref.shape[0]
    places = len(got) + 1
    rest = own_ref.shape[0]
    z = (coords_ref[0] >> 16) & 255
    held_ref[z] = term_ref[...]
    for k, ref in enumerate(got):
        held_ref[lax.rem(z + k + 1, places)] = ref[rest:]
    terms = jnp.sum(held_ref[...].astype(jnp.float32), axis=0).astype(out_ref.dtype)
    ahead, behind = got[places // 2 - 1], got[places // 2]
    for i in range(blocks):
        rows = pl.ds(i * side, side)
        total = own_ref[rows].astype(jnp.float32) + ahead[rows].astype(jnp.float32)
        out_ref[i, :side] = (total + behind[rows].astype(jnp.float32)).astype(out_ref.dtype)
        out_ref[i, side:] = terms


VMEM = pl.BlockSpec(memory_space=pltpu.VMEM)
SMEM = pl.BlockSpec(memory_space=pltpu.SMEM)
HBM = pl.BlockSpec(memory_space=pltpu.HBM)


def call(kernel, ins, outs, scratch, args, flops=0):
    return pl.pallas_call(
        kernel,
        out_shape=outs,
        in_specs=ins,
        out_specs=jax.tree.map(lambda _: VMEM, outs),
        scratch_shapes=scratch,
        compiler_params=pltpu.CompilerParams(vmem_limit_bytes=24 << 20),
        cost_estimate=pl.CostEstimate(
            flops=flops, transcendentals=0, bytes_accessed=4 * math.prod(outs[0].shape)
        ),
    )(*args)


def exchange(blocks, axes):
    return lax.all_to_all(blocks, axes, 0, 0, tiled=True)


def add(left, right):
    return (left.astype(jnp.float32) + right.astype(jnp.float32)).astype(jnp.bfloat16)


def swap_cores(value):
    return lax.ppermute(value, "c", [(0, 1), (1, 0)])


def on_device(features, weight1, weight2, tile_values, tile_coords, tile_count, out_grad):
    side, feat = features.shape[1], features.shape[2]
    z_n, yl_n = lax.axis_size("z"), lax.axis_size("yl")
    x_n, yh_n = lax.axis_size("x"), lax.axis_size("yh")
    rows_n, cols_n = z_n * yl_n, lax.axis_size(COL)
    half_n, middle = cols_n // 2, z_n // 2
    width = 2 * feat
    node_total = side * rows_n * cols_n
    slots = tile_values.shape[2]
    coords = (
        tile_coords[0, 0, 0]
        + (tile_coords[0, 0, 1] << 8)
        + (lax.axis_index("z").astype(jnp.int32) << 16)
        + (lax.axis_index("c").astype(jnp.int32) << 24)
    )
    dot = functools.partial(jnp.dot, preferred_element_type=jnp.float32)
    contract = (((0,), (0,)), ((), ()))
    bf16 = functools.partial(jax.ShapeDtypeStruct, dtype=jnp.bfloat16)
    f32 = functools.partial(jax.ShapeDtypeStruct, dtype=jnp.float32)
    tile_flops = 2 * side * side * width

    both = jnp.concatenate([features[0], out_grad[0]], axis=1)
    own = lax.all_gather(both, "yl", axis=0, tiled=True).reshape(yl_n, side, width)
    up = [(i, (i + 1) % z_n) for i in range(z_n)]
    down = [(i, (i - 1) % z_n) for i in range(z_n)]
    pieces = {0: own}
    for step in range(1, middle):
        pieces[-step % z_n] = lax.ppermute(pieces[(1 - step) % z_n], "z", up)
        pieces[step] = lax.ppermute(pieces[step - 1], "z", down)
    pieces[middle] = lax.ppermute(pieces[middle + 1], "z", up)
    block_rows, block_cols = tile_coords[0, 0, 0], tile_coords[0, 0, 1]
    z, core = (lax.axis_index(name).astype(jnp.int32) for name in ("z", "c"))
    source = ((block_cols // yl_n - z) % z_n) * yl_n + block_cols % yl_n
    row_place = (
        ((block_rows % 2) ^ core) * half_n
        + (block_rows // 2 % x_n) * yh_n
        + block_rows // (2 * x_n)
    )
    half = bf16((half_n, side, width))
    keep, send = pl.pallas_call(
        forward_kernel,
        out_shape=(half, half),
        in_specs=[SMEM] * 3 + [HBM] + [VMEM] * len(pieces),
        out_specs=(VMEM, VMEM),
        scratch_shapes=[
            pltpu.VMEM((slots, side, side), jnp.bfloat16),
            pltpu.VMEM((rows_n, side, width), jnp.bfloat16),
            pltpu.VMEM((cols_n + 1, side, width), jnp.float32),
            pltpu.SemaphoreType.DMA((slots // math.gcd(slots, UNROLL),)),
        ],
        compiler_params=pltpu.CompilerParams(vmem_limit_bytes=24 << 20),
        cost_estimate=pl.CostEstimate(
            flops=tile_flops * slots, transcendentals=0, bytes_accessed=2 * slots * side * side
        ),
    )(
        source,
        row_place,
        tile_count[0],
        pltpu.with_memory_space_constraint(tile_values[0, 0], pltpu.HBM),
        *(pieces[turn] for turn in range(z_n)),
    )

    pair = add(keep, swap_cores(send))
    got = exchange(pair, "x").reshape(x_n, yh_n * side, width)
    sums = jnp.sum(got.astype(jnp.float32), axis=0).astype(jnp.bfloat16)
    sums, coords = lax.optimization_barrier((sums, coords))
    swapped = lax.ppermute(sums, "yh", [(0, 1), (1, 0)])
    lists, list_sizes = pl.pallas_call(
        functools.partial(plan_kernel, (z_n, yl_n, yh_n, x_n)),
        out_shape=(
            jax.ShapeDtypeStruct((3 * slots + 1,), jnp.int32),
            jax.ShapeDtypeStruct((3,), jnp.int32),
        ),
        in_specs=[SMEM] * 2,
        out_specs=(SMEM, SMEM),
        compiler_params=pltpu.CompilerParams(vmem_limit_bytes=4 << 20),
        cost_estimate=pl.CostEstimate(flops=0, transcendentals=0, bytes_accessed=1 << 20),
    )(coords, tile_count[0])
    swapped, lists, list_sizes = lax.optimization_barrier((swapped, lists, list_sizes))
    plan = (lists, list_sizes, tile_values[0, 0])
    specs = [SMEM, SMEM, VMEM]
    sums = sums.astype(jnp.float32) + swapped.astype(jnp.float32)
    agg_one = sums[:, :feat].astype(jnp.bfloat16)
    agg_grad = sums[:, feat:].astype(jnp.bfloat16)
    pre_one = dot(agg_one, weight1)
    sigmoid = jax.nn.sigmoid(pre_one)
    hidden = (pre_one * sigmoid).astype(jnp.bfloat16)
    grad_hidden = dot(agg_grad, weight2.T)
    grad_pre = (grad_hidden * (sigmoid * (1.0 + pre_one * (1.0 - sigmoid)))).astype(jnp.bfloat16)
    grad_one = dot(grad_pre, weight1.T).astype(jnp.bfloat16)
    term_one = lax.dot_general(agg_one, grad_pre, contract, preferred_element_type=jnp.float32)
    term_two = lax.dot_general(hidden, agg_grad, contract, preferred_element_type=jnp.float32)

    both = jnp.concatenate([hidden, grad_one], axis=1)
    slices = jnp.concatenate([term_one, term_two], axis=1).astype(jnp.bfloat16)
    term_rows = feat // x_n
    slices = slices.reshape(x_n, term_rows, width)
    sent = jnp.concatenate(
        [jnp.broadcast_to(both[None], (x_n,) + both.shape), slices], axis=1
    )
    mine = exchange(sent, "x")
    theirs = swap_cores(mine)
    (begun,) = call(
        functools.partial(mine_kernel, yh_n),
        specs + [VMEM],
        (f32((rows_n + 1, side, width)),),
        [],
        (*plan, mine),
        tile_flops * slots // 2,
    )
    message = bf16((yl_n * side + term_rows, width))
    chunks = {}
    chunks[middle - 1], chunks[middle], terms = call(
        functools.partial(first_kernel, yh_n, (middle - 1) * yl_n),
        specs + [VMEM] * 3,
        (message, message, bf16((term_rows, width))),
        [pltpu.VMEM((2 * yl_n + 1, side, width), jnp.float32)],
        (*plan, mine, theirs, begun),
        tile_flops * slots // 8,
    )
    rest = tuple(k for k in range(z_n) if k not in chunks)
    outs = call(
        functools.partial(rest_kernel, yh_n, rest),
        specs + [VMEM] * 2,
        tuple(message if k else bf16((yl_n * side, width)) for k in rest),
        [pltpu.VMEM((rows_n + 1, side, width), jnp.float32)],
        (*plan, theirs, begun),
        tile_flops * slots // 2,
    )
    chunks.update(zip(rest, outs))

    ahead, behind = [], []
    down_sum, up_sum = chunks[middle], chunks[middle - 1]
    for step in range(middle):
        ahead.append(lax.ppermute(down_sum, "z", down))
        if step < middle - 1:
            behind.append(lax.ppermute(up_sum, "z", up))
            down_sum = add(ahead[-1], chunks[middle + 1 + step])
        if step < middle - 2:
            up_sum = add(behind[-1], chunks[middle - 2 - step])
    (sent,) = call(
        ring_sum_kernel,
        [SMEM] + [VMEM] * (z_n + 1),
        (bf16((yl_n, side + term_rows, width)),),
        [pltpu.VMEM((z_n, term_rows, width), jnp.bfloat16)],
        (coords, chunks[0], terms, *ahead, *behind[::-1]),
    )
    got = exchange(sent, "yl")
    terms = jnp.sum(got[:, side:].astype(jnp.float32), axis=0) * (1.0 / math.sqrt(node_total))
    weights = exchange(jnp.broadcast_to(terms[None], (x_n,) + terms.shape), "x")
    sums = jnp.sum(got[:, :side].astype(jnp.float32), axis=0).astype(jnp.bfloat16)
    output = dot(sums[:, :feat], weight2).astype(jnp.bfloat16)
    grad_features = sums[:, feat:]
    weights = weights.reshape(feat, width)
    return (output[None], grad_features[None], weights[:, :feat], weights[:, feat:])


def solution(mesh):
    fine = Mesh(mesh.devices.reshape(8, 4, 2, 4, 2), ("z", "yl", "yh", "x", "c"))
    placed = (
        P(COL, ROW, None),
        P(),
        P(),
        P(ROW, COL, None, None, None),
        P(ROW, COL, None, None),
        P(ROW, COL),
        P(COL, ROW, None),
    )
    return jax.shard_map(
        on_device,
        mesh=fine,
        in_specs=placed,
        out_specs=(P(COL, ROW, None), P(COL, ROW, None), P(), P()),
        check_vma=False,
    )
```

```python
import functools
import math

import jax
import jax.numpy as jnp
from jax import lax
from jax.experimental import pallas as pl
from jax.experimental.pallas import tpu as pltpu
from jax.sharding import Mesh, PartitionSpec as P

ROW = ("z", "yl")
COL = ("yh", "x", "c")
UNROLL = 32
MINE, FIRST, REST = range(3)


def add_slots(first, count, source_ref, target_ref, tiles_ref, panel_ref, acc_ref):
    spare = acc_ref.shape[0] - 1
    for k in range(tiles_ref.shape[0]):
        slot = first + k
        product = jnp.dot(
            tiles_ref[k], panel_ref[source_ref[slot]], preferred_element_type=jnp.float32
        )
        acc_ref[jnp.where(slot < count, target_ref[slot], spare)] += product


def forward_kernel(source_ref, target_ref, count_ref, tiles_ref, *refs):
    pieces, (keep_ref, send_ref, held_ref, panel_ref, acc_ref, sems) = refs[:-6], refs[-6:]
    steps = sems.shape[0]
    group = held_ref.shape[0] // steps
    copies = [
        pltpu.make_async_copy(
            tiles_ref.at[pl.ds(i * group, group)], held_ref.at[pl.ds(i * group, group)], sems.at[i]
        )
        for i in range(steps)
    ]
    for copy in copies:
        copy.start()
    acc_ref[...] = jnp.zeros_like(acc_ref)
    n = pieces[0].shape[0]
    for i, piece in enumerate(pieces):
        panel_ref[i * n : (i + 1) * n] = piece[...]
    count = count_ref[0]
    for i, copy in enumerate(copies):
        copy.wait()

        @pl.when(i * group < count)
        def _():
            tiles = held_ref.at[pl.ds(i * group, group)]
            add_slots(i * group, count, source_ref, target_ref, tiles, panel_ref, acc_ref)

    half = keep_ref.shape[0]
    keep_ref[...] = acc_ref[:half].astype(keep_ref.dtype)
    send_ref[...] = acc_ref[half : 2 * half].astype(send_ref.dtype)


def shift(value, n):
    return lax.shift_right_logical(value, jnp.int32(n.bit_length() - 1))


def plan_kernel(sizes, coords_ref, count_ref, list_ref, size_ref):
    z_n, yl_n, yh_n, x_n = sizes
    middle = z_n // 2
    slots, groups = coords_ref.shape[0], size_ref.shape[0]
    unroll = math.gcd(slots, 4)
    z, core, count = (coords_ref[0] >> 16) & 255, coords_ref[0] >> 24, count_ref[0]

    def step(first, ends):
        ends = list(ends)
        for k in range(unroll):
            slot = first * unroll + k
            row, col = coords_ref[slot] & 255, (coords_ref[slot] >> 8) & 255
            turn = (shift(col, yl_n) - z) & (z_n - 1)
            place = (shift(row, 2) & (x_n - 1)) * yh_n + shift(row, 2 * x_n)
            block = turn * yl_n + (col & (yl_n - 1))
            mine = (row & 1) == core
            chunks = (turn == middle) | (turn == middle - 1)
            group = jnp.where(mine, MINE, jnp.where(chunks, FIRST, REST))
            target = jnp.where(~mine & chunks, block - (middle - 1) * yl_n, block)
            at = jnp.int32(groups * slots)
            for g in range(groups):
                chosen = (slot < count) & (group == g)
                at = jnp.where(chosen, g * slots + ends[g], at)
                ends[g] = ends[g] + chosen.astype(jnp.int32)
            list_ref[at] = slot + (place << 8) + (target << 16)
        return tuple(ends)

    ends = lax.fori_loop(0, (count + unroll - 1) // unroll, step, (jnp.int32(0),) * groups)
    for group in range(groups):
        size_ref[group] = ends[group]


def add_tiles(unroll, group, list_ref, size_ref, tiles_ref, read, acc_ref):
    spare, slots = acc_ref.shape[0] - 1, tiles_ref.shape[0]
    contract = (((0,), (0,)), ((), ()))
    size = size_ref[group]

    def step(first, carry):
        for k in range(unroll):
            at = first * unroll + k
            live = at < size
            entry = list_ref[slots * group + jnp.minimum(at, slots - 1)]
            entry = jnp.where(live, entry, spare << 16)
            slot, source, target = entry & 255, (entry >> 8) & 255, entry >> 16
            product = lax.dot_general(
                tiles_ref[slot], read(source), contract, preferred_element_type=jnp.float32
            )
            acc_ref[target] += product
        return carry

    lax.fori_loop(0, (size + unroll - 1) // unroll, step, 0)


def reader(ref, side, held):
    def read(source):
        start = pl.multiple_of(lax.rem(source, held) * side, side)
        return ref[source // held, pl.ds(start, side), :]

    return read


def mine_kernel(held, list_ref, size_ref, tiles_ref, mine_ref, acc_ref):
    acc_ref[...] = jnp.zeros_like(acc_ref)
    read = reader(mine_ref, tiles_ref.shape[1], held)
    add_tiles(16, MINE, list_ref, size_ref, tiles_ref, read, acc_ref)


def first_kernel(
    held, begin, list_ref, size_ref, tiles_ref, mine_ref, theirs_ref, begun_ref,
    up_ref, down_ref, term_ref, acc_ref,
):
    side = tiles_ref.shape[1]
    blocks = acc_ref.shape[0] - 1
    acc_ref[:blocks] = begun_ref[begin : begin + blocks]
    acc_ref[blocks] = jnp.zeros_like(acc_ref[blocks])
    read = reader(theirs_ref, side, held)
    add_tiles(8, FIRST, list_ref, size_ref, tiles_ref, read, acc_ref)
    terms = jnp.sum(mine_ref[:, held * side :].astype(jnp.float32), axis=0) + jnp.sum(
        theirs_ref[:, held * side :].astype(jnp.float32), axis=0
    )
    terms = terms.astype(term_ref.dtype)
    term_ref[...] = terms
    for i in range(blocks // 2):
        rows = pl.ds(i * side, side)
        up_ref[rows] = acc_ref[i].astype(up_ref.dtype)
        down_ref[rows] = acc_ref[blocks // 2 + i].astype(down_ref.dtype)
    rest = blocks // 2 * side
    up_ref[rest:] = terms
    down_ref[rest:] = terms


def rest_kernel(held, turns, list_ref, size_ref, tiles_ref, theirs_ref, begun_ref, *refs):
    outs, acc_ref = refs[:-1], refs[-1]
    side = tiles_ref.shape[1]
    n = outs[0].shape[0] // side
    spare = acc_ref.shape[0] - 1
    acc_ref[spare] = jnp.zeros_like(acc_ref[spare])
    for turn in turns:
        acc_ref[turn * n : (turn + 1) * n] = begun_ref[turn * n : (turn + 1) * n]
    read = reader(theirs_ref, side, held)
    add_tiles(16, REST, list_ref, size_ref, tiles_ref, read, acc_ref)
    for turn, out_ref in zip(turns, outs):
        for i in range(n):
            out_ref[i * side : (i + 1) * side] = acc_ref[turn * n + i].astype(out_ref.dtype)
        if turn:
            out_ref[n * side :] = jnp.zeros_like(out_ref[n * side :])


def ring_sum_kernel(coords_ref, own_ref, term_ref, *refs):
    got, (out_ref, held_ref) = refs[:-2], refs[-2:]
    blocks, side = out_ref.shape[0], own_ref.shape[0] // out_ref.shape[0]
    places = len(got) + 1
    rest = own_ref.shape[0]
    z = (coords_ref[0] >> 16) & 255
    held_ref[z] = term_ref[...]
    for k, ref in enumerate(got):
        held_ref[lax.rem(z + k + 1, places)] = ref[rest:]
    terms = jnp.sum(held_ref[...].astype(jnp.float32), axis=0).astype(out_ref.dtype)
    ahead, behind = got[places // 2 - 1], got[places // 2]
    for i in range(blocks):
        rows = pl.ds(i * side, side)
        total = own_ref[rows].astype(jnp.float32) + ahead[rows].astype(jnp.float32)
        out_ref[i, :side] = (total + behind[rows].astype(jnp.float32)).astype(out_ref.dtype)
        out_ref[i, side:] = terms


VMEM = pl.BlockSpec(memory_space=pltpu.VMEM)
SMEM = pl.BlockSpec(memory_space=pltpu.SMEM)
HBM = pl.BlockSpec(memory_space=pltpu.HBM)


def call(kernel, ins, outs, scratch, args, flops=0):
    return pl.pallas_call(
        kernel,
        out_shape=outs,
        in_specs=ins,
        out_specs=jax.tree.map(lambda _: VMEM, outs),
        scratch_shapes=scratch,
        compiler_params=pltpu.CompilerParams(vmem_limit_bytes=24 << 20),
        cost_estimate=pl.CostEstimate(
            flops=flops, transcendentals=0, bytes_accessed=4 * math.prod(outs[0].shape)
        ),
    )(*args)


def exchange(blocks, axes):
    return lax.all_to_all(blocks, axes, 0, 0, tiled=True)


def add(left, right):
    return (left.astype(jnp.float32) + right.astype(jnp.float32)).astype(jnp.bfloat16)


def swap_cores(value):
    return lax.ppermute(value, "c", [(0, 1), (1, 0)])


def on_device(features, weight1, weight2, tile_values, tile_coords, tile_count, out_grad):
    side, feat = features.shape[1], features.shape[2]
    z_n, yl_n = lax.axis_size("z"), lax.axis_size("yl")
    x_n, yh_n = lax.axis_size("x"), lax.axis_size("yh")
    rows_n, cols_n = z_n * yl_n, lax.axis_size(COL)
    half_n, middle = cols_n // 2, z_n // 2
    width = 2 * feat
    node_total = side * rows_n * cols_n
    slots = tile_values.shape[2]
    coords = (
        tile_coords[0, 0, 0]
        + (tile_coords[0, 0, 1] << 8)
        + (lax.axis_index("z").astype(jnp.int32) << 16)
        + (lax.axis_index("c").astype(jnp.int32) << 24)
    )
    dot = functools.partial(jnp.dot, preferred_element_type=jnp.float32)
    contract = (((0,), (0,)), ((), ()))
    bf16 = functools.partial(jax.ShapeDtypeStruct, dtype=jnp.bfloat16)
    f32 = functools.partial(jax.ShapeDtypeStruct, dtype=jnp.float32)
    tile_flops = 2 * side * side * width

    both = jnp.concatenate([features[0], out_grad[0]], axis=1)
    own = lax.all_gather(both, "yl", axis=0, tiled=True).reshape(yl_n, side, width)
    up = [(i, (i + 1) % z_n) for i in range(z_n)]
    down = [(i, (i - 1) % z_n) for i in range(z_n)]
    pieces = {0: own}
    for step in range(1, middle):
        pieces[-step % z_n] = lax.ppermute(pieces[(1 - step) % z_n], "z", up)
        pieces[step] = lax.ppermute(pieces[step - 1], "z", down)
    pieces[middle] = lax.ppermute(pieces[middle + 1], "z", up)
    block_rows, block_cols = tile_coords[0, 0, 0], tile_coords[0, 0, 1]
    z, core = (lax.axis_index(name).astype(jnp.int32) for name in ("z", "c"))
    source = ((block_cols // yl_n - z) % z_n) * yl_n + block_cols % yl_n
    row_place = (
        ((block_rows % 2) ^ core) * half_n
        + (block_rows // 2 % x_n) * yh_n
        + block_rows // (2 * x_n)
    )
    half = bf16((half_n, side, width))
    keep, send = pl.pallas_call(
        forward_kernel,
        out_shape=(half, half),
        in_specs=[SMEM] * 3 + [HBM] + [VMEM] * len(pieces),
        out_specs=(VMEM, VMEM),
        scratch_shapes=[
            pltpu.VMEM((slots, side, side), jnp.bfloat16),
            pltpu.VMEM((rows_n, side, width), jnp.bfloat16),
            pltpu.VMEM((cols_n + 1, side, width), jnp.float32),
            pltpu.SemaphoreType.DMA((slots // math.gcd(slots, UNROLL),)),
        ],
        compiler_params=pltpu.CompilerParams(vmem_limit_bytes=24 << 20),
        cost_estimate=pl.CostEstimate(
            flops=tile_flops * slots, transcendentals=0, bytes_accessed=2 * slots * side * side
        ),
    )(
        source,
        row_place,
        tile_count[0],
        pltpu.with_memory_space_constraint(tile_values[0, 0], pltpu.HBM),
        *(pieces[turn] for turn in range(z_n)),
    )

    pair = add(keep, swap_cores(send))
    got = exchange(pair, "x").reshape(x_n, yh_n * side, width)
    sums = jnp.sum(got.astype(jnp.float32), axis=0).astype(jnp.bfloat16)
    sums, coords = lax.optimization_barrier((sums, coords))
    swapped = lax.ppermute(sums, "yh", [(0, 1), (1, 0)])
    lists, list_sizes = pl.pallas_call(
        functools.partial(plan_kernel, (z_n, yl_n, yh_n, x_n)),
        out_shape=(
            jax.ShapeDtypeStruct((3 * slots + 1,), jnp.int32),
            jax.ShapeDtypeStruct((3,), jnp.int32),
        ),
        in_specs=[SMEM] * 2,
        out_specs=(SMEM, SMEM),
        compiler_params=pltpu.CompilerParams(vmem_limit_bytes=4 << 20),
        cost_estimate=pl.CostEstimate(flops=0, transcendentals=0, bytes_accessed=1 << 20),
    )(coords, tile_count[0])
    swapped, lists, list_sizes = lax.optimization_barrier((swapped, lists, list_sizes))
    plan = (lists, list_sizes, tile_values[0, 0])
    specs = [SMEM, SMEM, VMEM]
    sums = sums.astype(jnp.float32) + swapped.astype(jnp.float32)
    agg_one = sums[:, :feat].astype(jnp.bfloat16)
    agg_grad = sums[:, feat:].astype(jnp.bfloat16)
    pre_one = dot(agg_one, weight1)
    sigmoid = jax.nn.sigmoid(pre_one)
    hidden = (pre_one * sigmoid).astype(jnp.bfloat16)
    grad_hidden = dot(agg_grad, weight2.T)
    grad_pre = (grad_hidden * (sigmoid * (1.0 + pre_one * (1.0 - sigmoid)))).astype(jnp.bfloat16)
    grad_one = dot(grad_pre, weight1.T).astype(jnp.bfloat16)
    term_one = lax.dot_general(agg_one, grad_pre, contract, preferred_element_type=jnp.float32)
    term_two = lax.dot_general(hidden, agg_grad, contract, preferred_element_type=jnp.float32)

    both = jnp.concatenate([hidden, grad_one], axis=1)
    slices = jnp.concatenate([term_one, term_two], axis=1).astype(jnp.bfloat16)
    term_rows = feat // x_n
    slices = slices.reshape(x_n, term_rows, width)
    sent = jnp.concatenate(
        [jnp.broadcast_to(both[None], (x_n,) + both.shape), slices], axis=1
    )
    mine = exchange(sent, "x")
    theirs = swap_cores(mine)
    (begun,) = call(
        functools.partial(mine_kernel, yh_n),
        specs + [VMEM],
        (f32((rows_n + 1, side, width)),),
        [],
        (*plan, mine),
        tile_flops * slots // 2,
    )
    message = bf16((yl_n * side + term_rows, width))
    chunks = {}
    chunks[middle - 1], chunks[middle], terms = call(
        functools.partial(first_kernel, yh_n, (middle - 1) * yl_n),
        specs + [VMEM] * 3,
        (message, message, bf16((term_rows, width))),
        [pltpu.VMEM((2 * yl_n + 1, side, width), jnp.float32)],
        (*plan, mine, theirs, begun),
        tile_flops * slots // 8,
    )
    rest = tuple(k for k in range(z_n) if k not in chunks)
    outs = call(
        functools.partial(rest_kernel, yh_n, rest),
        specs + [VMEM] * 2,
        tuple(message if k else bf16((yl_n * side, width)) for k in rest),
        [pltpu.VMEM((rows_n + 1, side, width), jnp.float32)],
        (*plan, theirs, begun),
        tile_flops * slots // 2,
    )
    chunks.update(zip(rest, outs))

    ahead, behind = [], []
    down_sum, up_sum = chunks[middle], chunks[middle - 1]
    for step in range(middle):
        ahead.append(lax.ppermute(down_sum, "z", down))
        if step < middle - 1:
            behind.append(lax.ppermute(up_sum, "z", up))
            down_sum = add(ahead[-1], chunks[middle + 1 + step])
        if step < middle - 2:
            up_sum = add(behind[-1], chunks[middle - 2 - step])
    (sent,) = call(
        ring_sum_kernel,
        [SMEM] + [VMEM] * (z_n + 1),
        (bf16((yl_n, side + term_rows, width)),),
        [pltpu.VMEM((z_n, term_rows, width), jnp.bfloat16)],
        (coords, chunks[0], terms, *ahead, *behind[::-1]),
    )
    got = exchange(sent, "yl")
    terms = jnp.sum(got[:, side:].astype(jnp.float32), axis=0) * (1.0 / math.sqrt(node_total))
    weights = exchange(jnp.broadcast_to(terms[None], (x_n,) + terms.shape), "x")
    sums = jnp.sum(got[:, :side].astype(jnp.float32), axis=0).astype(jnp.bfloat16)
    output = dot(sums[:, :feat], weight2).astype(jnp.bfloat16)
    grad_features = sums[:, feat:]
    weights = weights.reshape(feat, width)
    return (output[None], grad_features[None], weights[:, :feat], weights[:, feat:])


def solution(mesh):
    fine = Mesh(mesh.devices.reshape(8, 4, 2, 4, 2), ("z", "yl", "yh", "x", "c"))
    placed = (
        P(COL, ROW, None),
        P(),
        P(),
        P(ROW, COL, None, None, None),
        P(ROW, COL, None, None),
        P(ROW, COL),
        P(COL, ROW, None),
    )
    return jax.shard_map(
        on_device,
        mesh=fine,
        in_specs=placed,
        out_specs=(P(COL, ROW, None), P(COL, ROW, None), P(), P()),
        check_vma=False,
    )
```
